32 devices in a mesh: cuts: 2 (over y), wide: 8 (over z, x), narrow: 2 (over core).
Axes of the slice: x: 2, y: 2, z: 4, core: 2. Of those that a mesh axis runs over, the one named last changes fastest.
Arguments:
- stem_tensor: float32 [2, 4194304], P(None, ('cuts', 'wide', 'narrow')), parts along dimension 1, may hold values from -6 to 6
- sub_branches: bfloat16 [3, 2, 2, 512, 512], P(None, 'narrow', None, 'wide'), may hold values from -0.1875 to 0.1875
- branch_bits: int32 [3, 9], replicated, may hold values from 7 to 20, as said below
Outputs:
- amplitudes: float32 [2, 4194304], P(None, ('cuts', 'wide', 'narrow')), parts along dimension 1
The draws below stay inside these ranges and needn't reach their ends.
There are 2 independent parts, one for each index of `cuts`. The reference program is written for one: setup_inputs(seed, part) draws one part's arguments, and reference() takes and returns one part's arrays. A program takes and returns all parts, laid end to end along the dimension named above; an argument that names none is the same for every part. Nothing has to cross between parts.
Inputs may be any that keep to these rules, and one draw needn't show every extreme that they name: `branch_bits`: no bit below 7 is ever named. Row 0 holds 9 distinct bits of 7 to 16, bit 7 among them. Row 1 holds the 3 bits 17 + 1 to 20 and 6 distinct bits of 7 to 12. Row 2 holds bit 17 and 8 distinct bits of 7 to 12 and 18 to 20. Each row in any order.
All inputs are finite; a program needn't handle non-finite values.
Results may differ from the reference program's by a relative error of at most 0.005.
Values may be sent and summed in bfloat16 or wider, within the bound.
A program may use at most 64 MiB of HBM per device.

```python
import jax
import jax.numpy as jnp
from jax import lax

LBITS = 17
BBITS = 9
BRANCHES = 3
BDIM = 512
WBITS = 3
QBITS = 21
STEM = 2097152


def draw_branch_bits(key, part):
    subkeys = jax.random.split(key, 6)
    wide_positions = jnp.arange(LBITS + 1, LBITS + WBITS + 1, dtype=jnp.int32)
    first_pick = jax.random.permutation(subkeys[0], LBITS - 8)[:BBITS - 1].astype(jnp.int32) + 8
    first_set = jax.random.permutation(subkeys[1], jnp.concatenate([jnp.full((1,), 7, jnp.int32), first_pick]))
    low_pick = jax.random.permutation(subkeys[2], LBITS - WBITS - 8)[:BBITS - WBITS].astype(jnp.int32) + 7
    second_set = jax.random.permutation(subkeys[3], jnp.concatenate([wide_positions, low_pick]))
    third_pool = jnp.concatenate([jnp.arange(7, LBITS - WBITS - 1, dtype=jnp.int32), wide_positions])
    third_pick = third_pool[jax.random.permutation(subkeys[4], third_pool.shape[0])[:BBITS - 1]]
    third_set = jax.random.permutation(subkeys[5], jnp.concatenate([jnp.full((1,), LBITS, jnp.int32), third_pick]))
    return jnp.stack([first_set, second_set, third_set]).astype(jnp.int32)


def level_of(own_key, dims, shards, low, largest):
    def one(axis_at, blocks):
        heights = jax.random.uniform(jax.random.fold_in(jax.random.fold_in(own_key, 6), axis_at), (blocks,), jnp.float32, low / len(shards), largest / len(shards))
        return jnp.repeat(jnp.exp(heights), dims[axis_at] // blocks).reshape((-1,) + (1,) * (len(dims) - axis_at - 1))

    loudness = one(*shards[0])
    for cut in shards[1:]:
        loudness = loudness * one(*cut)
    return loudness


def gaussian(key, dims, width, limit, shards=(), kind=jnp.bfloat16):
    result = jax.random.normal(key, dims, jnp.float32) * width
    if len(shards) > 0:
        result = level_of(key, dims, shards, -0.22, 0.18) * result
    return jnp.clip(result, min=-limit, max=limit).astype(kind)


def setup_inputs(seed: int = 0, part: int = 0) -> dict:
    arg_keys = jax.random.split(jax.random.key(seed), 4)
    part_splits = jax.random.split(jax.random.fold_in(arg_keys[3], part), 4)
    return {
        "stem_tensor": gaussian(part_splits[0], (2, STEM), 1.0, 6.0, ((1, 16),), jnp.float32),
        "sub_branches": gaussian(arg_keys[1], (BRANCHES, 2, 2, BDIM, BDIM), (2 * BDIM) ** -0.5, 0.1875, ((1, 2), (3, 8))),
        "branch_bits": draw_branch_bits(jax.random.fold_in(arg_keys[3], 71), part),
    }


def bit_tables(chosen_bits, total_bits, width_bits):
    chosen_bits = chosen_bits.astype(jnp.int32)
    places = jnp.arange(total_bits, dtype=jnp.int32)
    orders = jnp.arange(width_bits, dtype=jnp.int32)
    matches = places[:, None] == chosen_bits[None, :]
    chosen = jnp.any(matches, axis=1)
    ranking = jnp.sum(jnp.where(matches, orders[None, :], 0), axis=1).astype(jnp.int32)
    unchosen = 1 - chosen.astype(jnp.int32)
    free_rank = (jnp.cumsum(unchosen) - unchosen).astype(jnp.int32)
    unit_ones = jnp.ones((total_bits,), jnp.int32)
    weight = jnp.where(chosen, jnp.left_shift(unit_ones, width_bits - 1 - ranking), jnp.left_shift(unit_ones, width_bits + free_rank))
    low_bits = total_bits // 2

    def partial_table(count, first_place, last_place):
        values = jnp.arange(count, dtype=jnp.int32)
        running = jnp.zeros((count,), jnp.int32)
        for position in range(first_place, last_place):
            running = running + jnp.bitwise_and(jnp.right_shift(values, position - first_place), 1) * weight[position]
        return running

    inverse = (partial_table(2 ** (total_bits - low_bits), low_bits, total_bits)[:, None] + partial_table(2 ** low_bits, 0, low_bits)[None, :]).reshape(-1)
    columns = jnp.arange(2 ** width_bits, dtype=jnp.int32)
    col_part = jnp.zeros((2 ** width_bits,), jnp.int32)
    for slot_no in range(width_bits):
        col_part = col_part + jnp.left_shift(jnp.bitwise_and(jnp.right_shift(columns, width_bits - 1 - slot_no), 1), chosen_bits[slot_no])
    row_ids = jnp.arange(2 ** (total_bits - width_bits), dtype=jnp.int32)
    row_part = jnp.zeros((2 ** (total_bits - width_bits),), jnp.int32)
    for position in range(total_bits):
        bit_value = jnp.bitwise_and(jnp.right_shift(row_ids, free_rank[position]), 1) * (2 ** position)
        row_part = row_part + jnp.where(chosen[position], 0, bit_value)
    gather_index = row_part[:, None] + col_part[None, :]
    return gather_index, inverse


def merge_branch(left_factor, right_factor):
    def half_product(first_matrix, second_matrix):
        return jnp.dot(first_matrix, second_matrix, preferred_element_type=jnp.float32)

    real_part = half_product(left_factor[0], right_factor[0]) - half_product(left_factor[1], right_factor[1])
    imag_part = half_product(left_factor[0], right_factor[1]) + half_product(left_factor[1], right_factor[0])
    return jnp.stack([real_part, imag_part]).astype(jnp.bfloat16)


def contract(amplitude, branch, gather_index, inverse):
    picked = jnp.take(amplitude, gather_index, axis=1)
    widened = branch.astype(jnp.float32)

    def real_product(data, matrix):
        return lax.dot_general(data, matrix, (((1,), (1,)), ((), ())), precision=lax.Precision.HIGHEST, preferred_element_type=jnp.float32)

    real_part = real_product(picked[0], widened[0]) - real_product(picked[1], widened[1])
    imag_part = real_product(picked[0], widened[1]) + real_product(picked[1], widened[0])
    merged = jnp.stack([real_part, imag_part]).reshape(2, -1)
    return jnp.take(merged, inverse, axis=1)


def reference(stem_tensor, sub_branches, branch_bits):
    amplitude = stem_tensor
    for which in range(BRANCHES):
        branch = merge_branch(sub_branches[which, 0], sub_branches[which, 1])
        gather_index, inverse = bit_tables(branch_bits[which], QBITS, BBITS)
        amplitude = contract(amplitude, branch, gather_index, inverse)
    return amplitude
```

```python
import functools

import jax
import jax.numpy as jnp
from jax import lax
from jax.experimental import pallas as pl
from jax.experimental.pallas import tpu as pltpu
from jax.sharding import PartitionSpec as P

LBITS = 17
BBITS = 9
BRANCHES = 3


lane_bits = 7
sublanes = 8
CORNERS_OVER_X = ((0, 2), (2, 0), (2, 2))
WHOLE_WAY = ()


def partner(value, axis, stride):
    mask = 2**stride
    pairs = [(source, source ^ mask) for source in range(lax.axis_size(axis))]
    return lax.ppermute(value, axis, pairs)


def bit_tables(chosen_bits, total_bits, width_bits):
    places = jnp.arange(total_bits, dtype=jnp.int32)
    orders = jnp.arange(width_bits, dtype=jnp.int32)
    matches = places[:, None] == chosen_bits[None, :]
    chosen = jnp.any(matches, axis=1)
    ranking = jnp.sum(jnp.where(matches, orders[None, :], 0), axis=1)
    unchosen = 1 - chosen.astype(jnp.int32)
    free_rank = jnp.cumsum(unchosen) - unchosen
    unit_ones = jnp.ones((total_bits,), jnp.int32)
    weight = jnp.where(
        chosen,
        jnp.left_shift(unit_ones, width_bits - 1 - ranking),
        jnp.left_shift(unit_ones, width_bits + free_rank),
    )
    low_bits = total_bits // 2

    def partial_table(count, first_place, last_place):
        values = jnp.arange(count, dtype=jnp.int32)
        running = jnp.zeros((count,), jnp.int32)
        for position in range(first_place, last_place):
            running = (
                running
                + jnp.bitwise_and(jnp.right_shift(values, position - first_place), 1)
                * weight[position]
            )
        return running

    inverse = (
        partial_table(2 ** (total_bits - low_bits), low_bits, total_bits)[:, None]
        + partial_table(2**low_bits, 0, low_bits)[None, :]
    ).reshape(-1)
    columns = jnp.arange(2**width_bits, dtype=jnp.int32)
    col_part = jnp.zeros((2**width_bits,), jnp.int32)
    for slot_no in range(width_bits):
        col_part = col_part + jnp.left_shift(
            jnp.bitwise_and(jnp.right_shift(columns, width_bits - 1 - slot_no), 1),
            chosen_bits[slot_no],
        )
    row_ids = jnp.arange(2 ** (total_bits - width_bits), dtype=jnp.int32)
    row_part = jnp.zeros((2 ** (total_bits - width_bits),), jnp.int32)
    for position in range(total_bits):
        bit_value = jnp.bitwise_and(jnp.right_shift(row_ids, free_rank[position]), 1) * 2**position
        row_part = row_part + jnp.where(chosen[position], 0, bit_value)
    gather_index = row_part[:, None] + col_part[None, :]
    return (gather_index, inverse)


def half_product(first_matrix, second_matrix):
    return jnp.dot(first_matrix, second_matrix, preferred_element_type=jnp.float32)


def merge_branch(left_factor, right_factor):
    real_part = half_product(left_factor[0], right_factor[0]) - half_product(
        left_factor[1], right_factor[1]
    )
    imag_part = half_product(left_factor[0], right_factor[1]) + half_product(
        left_factor[1], right_factor[0]
    )
    return jnp.stack([real_part, imag_part]).astype(jnp.bfloat16)


def contract_blocks(amplitude, branch, gather_index, inverse):
    lanes = 2**lane_bits
    blocks = amplitude.reshape(2, -1, lanes)
    picked = jnp.take(blocks, gather_index, axis=1)
    widened = branch.astype(jnp.float32)

    def real_product(data, matrix):
        return jnp.einsum(
            "rul,cu->rcl",
            data,
            matrix,
            precision=lax.Precision.HIGHEST,
            preferred_element_type=jnp.float32,
        )

    real_part = real_product(picked[0], widened[0]) - real_product(picked[1], widened[1])
    imag_part = real_product(picked[0], widened[1]) + real_product(picked[1], widened[0])
    merged = jnp.stack([real_part, imag_part]).reshape(2, -1, lanes)
    return jnp.take(merged, inverse, axis=1).reshape(2, -1)


def shards(stem_tensor, sub_branches, branch_bits):
    wide_count = lax.axis_size("wide")
    wide_log = wide_count.bit_length() - 1
    local_bits = LBITS
    block_shape = (2, wide_count, 2, stem_tensor.shape[1] // (2 * wide_count))
    leading = lax.axis_index("narrow") == 0

    def move_wide(amplitude):
        return lax.all_to_all(
            amplitude.reshape(block_shape), "wide", split_axis=1, concat_axis=1, tiled=True
        ).reshape(2, -1)

    def move_narrow(amplitude):
        return lax.all_to_all(
            amplitude.reshape(block_shape), "narrow", split_axis=2, concat_axis=2, tiled=True
        ).reshape(2, -1)

    def working_places(which):
        chosen_bits = branch_bits[which]
        if which == 0:
            return chosen_bits - lane_bits
        shifted = jnp.where(chosen_bits == local_bits, local_bits - wide_log - 1, chosen_bits)
        placed = jnp.where(chosen_bits > local_bits, chosen_bits - wide_log - 1, shifted)
        return placed - lane_bits

    amplitude = stem_tensor
    for which in range(BRANCHES):
        own_rows = sub_branches[which, 0]
        own_whole = lax.all_gather(own_rows, "wide", axis=1, tiled=True)
        partner_whole = partner(own_whole, "narrow", 0)
        branch = merge_branch(
            jnp.where(leading, own_whole, partner_whole),
            jnp.where(leading, partner_whole, own_whole),
        )
        if which == 1:
            amplitude = move_wide(amplitude)
        if which == 2:
            amplitude = move_narrow(amplitude)
        gather_index, inverse = bit_tables(working_places(which), local_bits - lane_bits, BBITS)
        amplitude = contract_blocks(amplitude, branch, gather_index, inverse)
    amplitude = move_narrow(amplitude)
    amplitude = move_wide(amplitude)
    return amplitude


MESH = pl.DeviceIdType.MESH


def xor(first, second):
    return first + second - 2 * first * second


def stem_kernel(
    count, places_ref, stem_ref, sub_ref, out_ref,
    xbuf, ybuf, bbuf, work, prod, turned, flipped, send_in, recv_in, send_out, recv_out, stem_held,
    stem_sem, own_sem, left_send, left_recv, right_send, right_recv, pair_send, pair_recv,
    relay_send, zb_send, zb_recv, xb_send, xb_recv, yb_send, yb_recv, pb_send, pb_recv,
    swap_send, swap_recv,
):
    wide = lax.axis_index("wide")
    narrow = lax.axis_index("narrow")
    cut = lax.axis_index("cuts")
    rows = sub_ref.shape[2]
    branches = sub_ref.shape[0]
    dim = bbuf.shape[2]
    quarter = dim // 4
    total = work.shape[0]
    lanes = work.shape[1] // 2
    bits = total.bit_length() - 1
    depth = count // 2
    z = wide // 2
    x = wide % 2
    members = 2 * count
    me = wide * 2 + narrow
    x_mate = 2 * z + 1 - x
    half = lanes // 2
    tiles = total // lanes

    stem_copy = pltpu.make_async_copy(stem_ref, stem_held, stem_sem)
    stem_copy.start()
    barrier = pltpu.get_barrier_semaphore()
    pl.semaphore_signal(barrier, inc=1, device_id={"cuts": 1 - cut}, device_id_type=MESH)
    for step in range(1, members):
        other = lax.rem(me + step, members)
        pl.semaphore_signal(
            barrier, inc=1, device_id={"wide": other // 2, "narrow": other % 2}, device_id_type=MESH
        )

    started = []
    call = functools.partial
    hops = range(depth)
    far_first = sorted(hops, key=lambda hop: -min(hop, depth - hop))

    def ahead(hop):
        return (z + hop) % depth

    side = z // (depth // 2)
    partner = z + 1 - 2 * (z % 2)
    inner = (z + side) % 2
    level_of = (z, partner, depth // 2 - side, (depth - 1) * (1 - side))
    far_class = 3 - inner
    class_of = (0, 1, far_class, far_class)
    relays = inner == 1

    def row_span(block):
        return pl.ds(pl.multiple_of(block * rows, rows), rows)

    def column_span(block):
        return pl.ds(pl.multiple_of(block * quarter, quarter), quarter)

    def remote(src, dst, send_sem, recv_sem, device_id):
        return pltpu.make_async_remote_copy(
            src_ref=src, dst_ref=dst, send_sem=send_sem, recv_sem=recv_sem,
            device_id=device_id, device_id_type=MESH,
        )

    def guarded(guard, action):
        if guard is None:
            action()
        else:
            pl.when(guard)(action)

    def launch(build, guard=None):
        guarded(guard, lambda: build().start())
        started.append((build, guard))

    def await_recv(build, guard=None):
        guarded(guard, lambda: build().wait_recv())

    holds_left = narrow == 0
    holds_right = narrow == 1
    other_core = {"narrow": 1 - narrow}
    own_columns = column_span(2 * x + cut)

    def left_exchange(which):
        return remote(
            sub_ref.at[which], xbuf.at[which], left_send.at[which], left_recv.at[which],
            {"wide": x_mate, "narrow": 1 - narrow},
        )

    def right_copy(which, across, kind):
        to_x = 1 - x if across else x
        return remote(
            sub_ref.at[which, :, :, column_span(2 * to_x + cut)], ybuf.at[which, :, row_span(wide)],
            right_send.at[which, across, kind], right_recv.at[which, class_of[kind]],
            {"wide": 2 * level_of[kind] + to_x, "narrow": 1 - across},
        )

    def right_block(which, kind):
        return ybuf.at[which, :, row_span(2 * level_of[kind] + xor(x, 1 - narrow))]

    def right_relay(which, kind):
        block = right_block(which, kind)
        return remote(
            block, block, relay_send.at[0, which, kind], right_recv.at[which, kind], {"wide": 2 * partner + x}
        )

    def left_own(which):
        return pltpu.make_async_copy(sub_ref.at[which], xbuf.at[which], own_sem.at[which])

    def right_own(which):
        return pltpu.make_async_copy(
            sub_ref.at[which, :, :, own_columns], ybuf.at[which, :, row_span(wide)], own_sem.at[which]
        )

    def pair_copy(which, hop):
        block = right_block(which, hop)
        return remote(block, block, pair_send.at[which, hop], pair_recv.at[which, hop], other_core)

    def b_block(which, level, far_x, far_cut):
        from_x = 1 - x if far_x else x
        from_cut = 1 - cut if far_cut else cut
        return bbuf.at[
            which, :, row_span(2 * level + xor(from_x, narrow)), column_span(2 * from_x + from_cut)
        ]

    def zb_copy(which, kind):
        block = b_block(which, z, 0, 0)
        return remote(
            block, block, zb_send.at[which, kind], zb_recv.at[which, class_of[kind]],
            {"wide": 2 * level_of[kind] + x},
        )

    def zb_relay(which, kind):
        block = b_block(which, level_of[kind], 0, 0)
        return remote(
            block, block, relay_send.at[1, which, kind], zb_recv.at[which, kind], {"wide": 2 * partner + x}
        )

    def xb_copy(which, far_cut, hop):
        block = b_block(which, level_of[hop], 0, far_cut)
        return remote(
            block, block, xb_send.at[which, far_cut, hop], xb_recv.at[which, far_cut, hop], {"wide": x_mate}
        )

    def yb_copy(which, far_x, hop):
        block = b_block(which, level_of[hop], far_x, 0)
        return remote(
            block, block, yb_send.at[which, far_x, hop], yb_recv.at[which, far_x, hop], {"cuts": 1 - cut}
        )

    def pb_copy(which, far_x, far_cut, hop):
        block = b_block(which, level_of[hop], far_x, far_cut)
        return remote(
            block, block, pb_send.at[which, far_x, far_cut, hop], pb_recv.at[which, far_x, far_cut, hop],
            other_core,
        )

    def open_exchange(which):
        launch(call(left_exchange, which), holds_left)
        guarded(holds_left, lambda: left_own(which).start())
        for kind in (3, 2, 1, 0) if which in WHOLE_WAY else (2, 1, 0):
            launch(call(right_copy, which, 1, kind), holds_right)
            if kind:
                launch(call(right_copy, which, 0, kind), holds_right)
        guarded(holds_right, lambda: right_own(which).start())

    def merge(which):
        guarded(holds_left, lambda: left_own(which).wait())
        await_recv(call(left_exchange, which), holds_right)
        for hop in hops:
            await_recv(call(pair_copy, which, hop))
        left = jnp.concatenate([xbuf[which, part] for part in range(2)], axis=0)
        right = jnp.concatenate([ybuf[which, part] for part in range(2)], axis=1)
        both = jnp.dot(left, right, preferred_element_type=jnp.float32)
        real = both[:rows, :quarter] - both[rows:, quarter:]
        imag = both[:rows, quarter:] + both[rows:, :quarter]
        span = row_span(2 * z + xor(x, narrow))
        bbuf[which, 0, span, own_columns] = real.astype(jnp.bfloat16)
        bbuf[which, 1, span, own_columns] = imag.astype(jnp.bfloat16)
        for kind in (2, 1):
            launch(call(zb_copy, which, kind))
        spread(which, 0)

    def spread(which, hop):
        launch(call(yb_copy, which, 0, hop))
        launch(call(xb_copy, which, 0, hop))
        launch(call(pb_copy, which, 0, 0, hop))

    def over_x(which, hop):
        return (hop, which) in CORNERS_OVER_X

    def take_xb(which, far_cut, hop):
        await_recv(call(xb_copy, which, far_cut, hop))
        if not far_cut and not over_x(which, hop):
            launch(call(yb_copy, which, 1, hop))
        launch(call(pb_copy, which, 1, far_cut, hop))

    def take_yb(which, far_x, hop):
        await_recv(call(yb_copy, which, far_x, hop))
        if not far_x and over_x(which, hop):
            launch(call(xb_copy, which, 1, hop))
        launch(call(pb_copy, which, far_x, 1, hop))

    def take_sides(which, hop):
        take_xb(which, 0, hop)
        take_yb(which, 0, hop)

    def take_corner(which, hop):
        if over_x(which, hop):
            take_xb(which, 1, hop)
        else:
            take_yb(which, 1, hop)

    def take_right_piece(which, hop):
        if hop == 0:
            guarded(holds_right, lambda: right_own(which).wait())
            await_recv(call(right_copy, which, 1, 0), holds_left)
        else:
            await_recv(call(right_relay, which, hop))
            if hop > 1 and which not in WHOLE_WAY:
                launch(call(right_relay, which, hop), relays)
        launch(call(pair_copy, which, hop))

    def take_z(which, hop):
        await_recv(call(zb_relay, which, hop))
        if hop > 1:
            launch(call(zb_relay, which, hop), relays)
        spread(which, hop)

    near_first = list(reversed(far_first))

    def complete(which):
        for hop in hops:
            for far_x in (0, 1):
                for far_cut in (0, 1):
                    await_recv(call(pb_copy, which, far_x, far_cut, hop))

    width = dim.bit_length() - 1
    narrow_place = bits - 1 - (count.bit_length() - 1)

    def named_place(which, slot):
        bit = places_ref[which, slot]
        return bit + jnp.where(bit < LBITS, -lane_bits, narrow_place - LBITS)

    places = [[named_place(which, slot) for slot in range(width)] for which in range(branches)]

    def free_place(which):
        rest = bits * (bits - 1) // 2
        for slot in range(width):
            rest = rest - places[which][slot]
        return rest

    def bit_at(values, position):
        return jnp.bitwise_and(jnp.right_shift(values, position), 1)

    def gathered_place(which, values):
        found = jnp.left_shift(bit_at(values, free_place(which)), width)
        for slot in range(width):
            found = found + jnp.left_shift(
                bit_at(values, places[which][slot]), width - 1 - slot
            )
        return found

    def natural_place(which, values):
        found = jnp.left_shift(bit_at(values, width), free_place(which))
        for slot in range(width):
            found = found + jnp.left_shift(
                bit_at(values, width - 1 - slot), places[which][slot]
            )
        return found

    step = min(256, total)
    line = lax.broadcasted_iota(jnp.int32, (1, total), 1)

    def onehot(first, size, goal):
        index = lax.broadcasted_iota(jnp.int32, (size, total), 0) + first
        return (index == goal).astype(jnp.float32).astype(jnp.bfloat16)

    def product(left, right, left_axis, right_axis):
        return lax.dot_general(
            left, right, (((left_axis,), (right_axis,)), ((), ())),
            preferred_element_type=jnp.float32,
        )

    def permute(source, source_axis, goal):
        for first in range(0, total, step):
            work[first:first + step, :] = product(
                onehot(first, step, goal), source, 1, source_axis
            ).astype(jnp.bfloat16)

    def contract(which):
        branch = jnp.concatenate([bbuf[which, part] for part in range(2)], axis=1)
        for first in range(0, total, dim):
            data = work[first:first + dim, :]
            spun = jnp.concatenate([-data[:, lanes:], data[:, :lanes]], axis=1)
            both = jnp.concatenate([data, spun], axis=0)
            prod[first:first + dim, :] = jnp.dot(
                branch, both, preferred_element_type=jnp.float32
            ).astype(jnp.bfloat16)

    def swap_targets(round_no, hop):
        source, target = ((send_in, recv_in), (send_out, recv_out))[round_no]
        piece = source.shape[0] // members
        for turn in range(4):
            across, other_side = turn // 2, turn % 2
            if hop == 0 and turn == 0:
                continue
            to_x = x if across == 0 else 1 - x
            to_core = narrow if other_side == 0 else 1 - narrow
            to_wide = 2 * ahead(hop) + to_x
            other = 2 * to_wide + to_core
            yield remote(
                source.at[pl.ds(pl.multiple_of(other * piece, piece), piece)],
                target.at[pl.ds(pl.multiple_of(me * piece, piece), piece)],
                swap_send.at[round_no, 4 * hop + turn],
                swap_recv.at[round_no, 4 * hop + turn],
                {"wide": to_wide, "narrow": to_core},
            )

    def swap_start(round_no, hop):
        for copy in swap_targets(round_no, hop):
            copy.start()

    def swap_wait(round_no):
        for hop in far_first:
            for copy in swap_targets(round_no, hop):
                copy.wait_recv()

    def keep_own(source, target):
        piece = source.shape[0] // members
        mine = pl.ds(pl.multiple_of(me * piece, piece), piece)
        target[mine, :] = source[mine, :]

    def pack():
        sides = [
            stem_held[pl.ds(part, total, stride=2), :].T.reshape(members, 1, sublanes, total)
            for part in range(2)
        ]
        send_in[...] = jnp.concatenate(sides, axis=1).reshape(2 * lanes, total).astype(jnp.bfloat16)
        keep_own(send_in, recv_in)

    def arrange():
        blocks = recv_in[...].astype(jnp.float32).reshape(members, 2, sublanes, total)
        return jnp.concatenate(
            [blocks[:, part].reshape(lanes, total) for part in range(2)], axis=0
        ).astype(jnp.bfloat16)

    def mix(low, high):
        return (
            jnp.concatenate([low[..., :half], high[..., :half]], axis=-1),
            jnp.concatenate([low[..., half:], high[..., half:]], axis=-1),
        )

    def turn_over():
        goal = natural_place(0, line)
        for first in range(0, total, step):
            turned[:, first:first + step] = product(prod[...], onehot(first, step, goal), 0, 1)
        for tile in range(tiles):
            block = turned[:, tile * lanes:(tile + 1) * lanes].reshape(2, count, 2, sublanes, lanes)
            for side, mixed in enumerate(mix(block[:, :, 0], block[:, :, 1])):
                for part in range(2):
                    first = ((part * 2 + side) * tiles + tile) * sublanes
                    flipped[first:first + sublanes, :] = jnp.concatenate(
                        [mixed[part, column] for column in range(count)], axis=1
                    )

    def hand_out(hop, goal):
        span = 2 * lanes
        first = ahead(hop) * span
        level = product(prod[...], onehot(first, span, goal), 0, 1)
        piece = send_out.shape[0] // members
        for to_x in range(2):
            block = level[:, to_x * lanes:(to_x + 1) * lanes].reshape(2, 2, half, lanes)
            for side, mixed in enumerate(mix(block[:, 0], block[:, 1])):
                other = 2 * (2 * ahead(hop) + to_x) + side
                send_out[pl.ds(pl.multiple_of(other * piece, piece), piece), :] = mixed.reshape(
                    piece, lanes
                ).astype(jnp.bfloat16)
        swap_start(1, hop)

    def write():
        for tile in range(tiles):
            for part in range(2):
                first = (part * tiles + tile) * sublanes
                block = jnp.concatenate(
                    [
                        recv_out[
                            member * lanes + first // 16 * 16:member * lanes + first // 16 * 16 + 16, :
                        ].astype(jnp.float32)[first % 16:first % 16 + sublanes]
                        for member in range(members)
                    ],
                    axis=0,
                )
                out_ref[pl.ds(2 * tile * lanes + part, lanes, stride=2), :] = block.T

    stem_copy.wait()
    pack()
    pl.semaphore_wait(barrier, members)
    swap_start(0, 1)
    open_exchange(1)
    take_right_piece(1, 0)
    open_exchange(0)
    open_exchange(2)
    take_right_piece(1, 3)
    take_right_piece(1, 2)
    take_right_piece(1, 1)
    merge(1)
    take_right_piece(0, 0)
    take_right_piece(0, 1)
    take_right_piece(0, 3)
    take_right_piece(0, 2)
    take_right_piece(2, 1)
    take_right_piece(2, 0)
    merge(0)
    take_right_piece(2, 2)
    take_right_piece(2, 3)
    take_z(1, 2)
    merge(2)
    take_z(0, 2)
    take_z(1, 3)
    take_sides(0, 0)
    take_z(2, 2)
    take_z(1, 1)
    take_sides(1, 2)
    take_z(0, 3)
    take_sides(0, 2)
    take_z(0, 1)
    take_sides(2, 2)
    take_sides(1, 3)
    take_z(2, 1)
    swap_start(0, 2)
    take_sides(1, 0)
    take_sides(1, 1)
    take_corner(0, 0)
    take_z(2, 3)
    take_corner(0, 2)
    swap_start(0, 3)
    swap_start(0, 0)
    take_sides(0, 1)
    take_sides(0, 3)
    take_sides(2, 1)
    take_corner(0, 1)
    take_corner(1, 0)
    take_sides(2, 0)
    take_corner(0, 3)
    take_corner(2, 2)
    take_sides(2, 3)
    take_corner(1, 1)
    take_corner(2, 1)
    take_corner(1, 2)
    take_corner(1, 3)
    complete(0)
    swap_wait(0)
    permute(arrange(), 1, gathered_place(0, line))
    contract(0)
    turn_over()
    take_corner(2, 3)
    take_corner(2, 0)
    complete(1)
    permute(flipped[...].astype(jnp.bfloat16), 1, gathered_place(1, line))
    contract(1)
    permute(prod[...], 0, gathered_place(2, natural_place(1, line)))
    complete(2)
    contract(2)
    goal = natural_place(2, line)
    for hop in far_first:
        hand_out(hop, goal)
    keep_own(send_out, recv_out)
    swap_wait(1)
    write()


    for hop in hops:
        for round_no in range(2):
            for copy in swap_targets(round_no, hop):
                copy.wait_send()
    for build, guard in started:
        guarded(guard, lambda: build().wait_send())


def shards_in_kernel(stem_tensor, sub_branches, branch_bits):
    count = lax.axis_size("wide")
    depth = count // 2
    lanes = 2**lane_bits
    total = stem_tensor.shape[1] // lanes
    dim = sub_branches.shape[-1]
    stem = stem_tensor.reshape(2, total, lanes).transpose(1, 0, 2).reshape(2 * total, lanes)
    vmem = pl.BlockSpec(memory_space=pltpu.VMEM)
    hbm = pl.BlockSpec(memory_space=pl.ANY)
    each = (BRANCHES, depth)
    semaphores = [pltpu.SemaphoreType.DMA(()), pltpu.SemaphoreType.DMA((BRANCHES,))]
    for sent, received in (
        ((BRANCHES,), (BRANCHES,)), ((BRANCHES, 2, depth), each), (each, each), (each, each),
        ((BRANCHES, 2, depth),) * 2, ((BRANCHES, 2, depth),) * 2, ((BRANCHES, 2, 2, depth),) * 2, ((2, 2 * count),) * 2,
    ):
        semaphores += [pltpu.SemaphoreType.DMA(sent), pltpu.SemaphoreType.DMA(received)]
    semaphores.insert(8, pltpu.SemaphoreType.DMA((2,) + each))
    half_size = jnp.bfloat16
    result = pl.pallas_call(
        functools.partial(stem_kernel, count),
        out_shape=jax.ShapeDtypeStruct((2 * total, lanes), jnp.float32),
        in_specs=[pl.BlockSpec(memory_space=pltpu.SMEM), hbm, hbm],
        out_specs=vmem,
        scratch_shapes=[
            pltpu.VMEM((BRANCHES,) + sub_branches.shape[2:], half_size),
            pltpu.VMEM((BRANCHES, 2, dim, dim // 4), half_size),
            pltpu.VMEM((BRANCHES, 2, dim, dim), half_size),
            pltpu.VMEM((total, 2 * lanes), half_size),
            pltpu.VMEM((total, 2 * lanes), half_size),
            pltpu.VMEM((2 * lanes, total), jnp.float32),
            pltpu.VMEM((2 * lanes, total), jnp.float32),
            pltpu.VMEM((2 * lanes, total), half_size),
            pltpu.VMEM((2 * lanes, total), half_size),
            pltpu.VMEM((2 * total, lanes), half_size),
            pltpu.VMEM((2 * total, lanes), half_size),
            pltpu.VMEM((2 * total, lanes), jnp.float32),
        ] + semaphores,
        compiler_params=pltpu.CompilerParams(collective_id=0, has_side_effects=True),
    )(branch_bits, stem, sub_branches[:, 0])
    return result.reshape(total, 2, lanes).transpose(1, 0, 2).reshape(2, -1)


sublane_tile = 16


def solution(mesh):
    in_specs = (P(None, ("cuts", "wide", "narrow")), P(None, "narrow", None, "wide", None), P())
    out_specs = P(None, ("cuts", "wide", "narrow"))

    def run(stem_tensor, sub_branches, branch_bits):
        whole_tiles = sub_branches.shape[3] % sublane_tile == 0 and mesh.shape["cuts"] == 2
        whole_groups = 2 * mesh.shape["wide"] * sublanes == 2**lane_bits
        body = shards_in_kernel if whole_tiles and whole_groups else shards
        return body(stem_tensor, sub_branches, branch_bits)

    return jax.shard_map(run, mesh=mesh, in_specs=in_specs, out_specs=out_specs, check_vma=False)
```

```python
import functools

import jax
import jax.numpy as jnp
from jax import lax
from jax.experimental import pallas as pl
from jax.experimental.pallas import tpu as pltpu
from jax.sharding import PartitionSpec as P

LBITS = 17
BBITS = 9
BRANCHES = 3


lane_bits = 7
sublanes = 8
kernel_vmem = 32 * 2**20
CORNERS_OVER_X = ((2, 0), (2, 2))
WHOLE_WAY = ()
SIDEWAYS_FIRST = ()
CORNERS_DIRECT = ()
LEVELS_DIRECT = ()


def partner(value, axis, stride):
    mask = 2**stride
    pairs = [(source, source ^ mask) for source in range(lax.axis_size(axis))]
    return lax.ppermute(value, axis, pairs)


def bit_tables(chosen_bits, total_bits, width_bits):
    places = jnp.arange(total_bits, dtype=jnp.int32)
    orders = jnp.arange(width_bits, dtype=jnp.int32)
    matches = places[:, None] == chosen_bits[None, :]
    chosen = jnp.any(matches, axis=1)
    ranking = jnp.sum(jnp.where(matches, orders[None, :], 0), axis=1)
    unchosen = 1 - chosen.astype(jnp.int32)
    free_rank = jnp.cumsum(unchosen) - unchosen
    unit_ones = jnp.ones((total_bits,), jnp.int32)
    weight = jnp.where(
        chosen,
        jnp.left_shift(unit_ones, width_bits - 1 - ranking),
        jnp.left_shift(unit_ones, width_bits + free_rank),
    )
    low_bits = total_bits // 2

    def partial_table(count, first_place, last_place):
        values = jnp.arange(count, dtype=jnp.int32)
        running = jnp.zeros((count,), jnp.int32)
        for position in range(first_place, last_place):
            running = (
                running
                + jnp.bitwise_and(jnp.right_shift(values, position - first_place), 1)
                * weight[position]
            )
        return running

    inverse = (
        partial_table(2 ** (total_bits - low_bits), low_bits, total_bits)[:, None]
        + partial_table(2**low_bits, 0, low_bits)[None, :]
    ).reshape(-1)
    columns = jnp.arange(2**width_bits, dtype=jnp.int32)
    col_part = jnp.zeros((2**width_bits,), jnp.int32)
    for slot_no in range(width_bits):
        col_part = col_part + jnp.left_shift(
            jnp.bitwise_and(jnp.right_shift(columns, width_bits - 1 - slot_no), 1),
            chosen_bits[slot_no],
        )
    row_ids = jnp.arange(2 ** (total_bits - width_bits), dtype=jnp.int32)
    row_part = jnp.zeros((2 ** (total_bits - width_bits),), jnp.int32)
    for position in range(total_bits):
        bit_value = jnp.bitwise_and(jnp.right_shift(row_ids, free_rank[position]), 1) * 2**position
        row_part = row_part + jnp.where(chosen[position], 0, bit_value)
    gather_index = row_part[:, None] + col_part[None, :]
    return (gather_index, inverse)


def half_product(first_matrix, second_matrix):
    return jnp.dot(first_matrix, second_matrix, preferred_element_type=jnp.float32)


def merge_branch(left_factor, right_factor):
    real_part = half_product(left_factor[0], right_factor[0]) - half_product(
        left_factor[1], right_factor[1]
    )
    imag_part = half_product(left_factor[0], right_factor[1]) + half_product(
        left_factor[1], right_factor[0]
    )
    return jnp.stack([real_part, imag_part]).astype(jnp.bfloat16)


def contract_blocks(amplitude, branch, gather_index, inverse):
    lanes = 2**lane_bits
    blocks = amplitude.reshape(2, -1, lanes)
    picked = jnp.take(blocks, gather_index, axis=1)
    widened = branch.astype(jnp.float32)

    def real_product(data, matrix):
        return jnp.einsum(
            "rul,cu->rcl",
            data,
            matrix,
            precision=lax.Precision.HIGHEST,
            preferred_element_type=jnp.float32,
        )

    real_part = real_product(picked[0], widened[0]) - real_product(picked[1], widened[1])
    imag_part = real_product(picked[0], widened[1]) + real_product(picked[1], widened[0])
    merged = jnp.stack([real_part, imag_part]).reshape(2, -1, lanes)
    return jnp.take(merged, inverse, axis=1).reshape(2, -1)


def shards(stem_tensor, sub_branches, branch_bits):
    wide_count = lax.axis_size("wide")
    wide_log = wide_count.bit_length() - 1
    local_bits = LBITS
    block_shape = (2, wide_count, 2, stem_tensor.shape[1] // (2 * wide_count))
    leading = lax.axis_index("narrow") == 0

    def move_wide(amplitude):
        return lax.all_to_all(
            amplitude.reshape(block_shape), "wide", split_axis=1, concat_axis=1, tiled=True
        ).reshape(2, -1)

    def move_narrow(amplitude):
        return lax.all_to_all(
            amplitude.reshape(block_shape), "narrow", split_axis=2, concat_axis=2, tiled=True
        ).reshape(2, -1)

    def working_places(which):
        chosen_bits = branch_bits[which]
        if which == 0:
            return chosen_bits - lane_bits
        shifted = jnp.where(chosen_bits == local_bits, local_bits - wide_log - 1, chosen_bits)
        placed = jnp.where(chosen_bits > local_bits, chosen_bits - wide_log - 1, shifted)
        return placed - lane_bits

    amplitude = stem_tensor
    for which in range(BRANCHES):
        own_rows = sub_branches[which, 0]
        own_whole = lax.all_gather(own_rows, "wide", axis=1, tiled=True)
        partner_whole = partner(own_whole, "narrow", 0)
        branch = merge_branch(
            jnp.where(leading, own_whole, partner_whole),
            jnp.where(leading, partner_whole, own_whole),
        )
        if which == 1:
            amplitude = move_wide(amplitude)
        if which == 2:
            amplitude = move_narrow(amplitude)
        gather_index, inverse = bit_tables(working_places(which), local_bits - lane_bits, BBITS)
        amplitude = contract_blocks(amplitude, branch, gather_index, inverse)
    amplitude = move_narrow(amplitude)
    amplitude = move_wide(amplitude)
    return amplitude


MESH = pl.DeviceIdType.MESH


def xor(first, second):
    return first + second - 2 * first * second


def stem_kernel(
    count, bits_ref, stem_ref, sub_ref, out_ref, places_ref, places_sem,
    xbuf, ybuf, bbuf, work, prod, turned, flipped, send_in, recv_in, send_out, recv_out, stem_held,
    stem_sem, own_sem, left_send, left_recv, right_send, right_recv, pair_send, pair_recv,
    relay_send, zb_send, zb_recv, xb_send, xb_recv, yb_send, yb_recv, pb_send, pb_recv,
    swap_send, swap_recv,
):
    wide = lax.axis_index("wide")
    narrow = lax.axis_index("narrow")
    cut = lax.axis_index("cuts")
    rows = sub_ref.shape[2]
    branches = sub_ref.shape[0]
    dim = bbuf.shape[2]
    quarter = dim // 4
    total = work.shape[0]
    lanes = work.shape[1] // 2
    bits = total.bit_length() - 1
    depth = count // 2
    z = wide // 2
    x = wide % 2
    members = 2 * count
    me = wide * 2 + narrow
    x_mate = 2 * z + 1 - x
    half = lanes // 2
    tiles = total // lanes

    stem_copy = pltpu.make_async_copy(stem_ref, stem_held, stem_sem)
    stem_copy.start()
    places_copy = pltpu.make_async_copy(bits_ref, places_ref, places_sem)
    places_copy.start()
    barrier = pltpu.get_barrier_semaphore()
    corner = {"wide": x_mate, "cuts": 1 - cut}
    for target in ({"cuts": 1 - cut}, corner):
        pl.semaphore_signal(barrier, inc=1, device_id=target, device_id_type=MESH)
    for step in range(1, members):
        other = lax.rem(me + step, members)
        pl.semaphore_signal(
            barrier, inc=1, device_id={"wide": other // 2, "narrow": other % 2}, device_id_type=MESH
        )

    started = []
    call = functools.partial
    hops = range(depth)
    far_first = sorted(hops, key=lambda hop: -min(hop, depth - hop))

    def ahead(hop):
        return (z + hop) % depth

    side = z // (depth // 2)
    partner = z + 1 - 2 * (z % 2)
    inner = (z + side) % 2
    level_of = (z, partner, depth // 2 - side, (depth - 1) * (1 - side))
    far_class = 3 - inner
    class_of = (0, 1, far_class, far_class)
    relays = inner == 1

    def row_span(block):
        return pl.ds(pl.multiple_of(block * rows, rows), rows)

    def column_span(block):
        return pl.ds(pl.multiple_of(block * quarter, quarter), quarter)

    def remote(src, dst, send_sem, recv_sem, device_id):
        return pltpu.make_async_remote_copy(
            src_ref=src, dst_ref=dst, send_sem=send_sem, recv_sem=recv_sem,
            device_id=device_id, device_id_type=MESH,
        )

    def guarded(guard, action):
        if guard is None:
            action()
        else:
            pl.when(guard)(action)

    def launch(build, guard=None):
        guarded(guard, lambda: build().start())
        started.append((build, guard))

    def await_recv(build, guard=None):
        guarded(guard, lambda: build().wait_recv())

    holds_left = narrow == 0
    holds_right = narrow == 1
    other_core = {"narrow": 1 - narrow}
    own_columns = column_span(2 * x + cut)

    def left_exchange(which):
        return remote(
            sub_ref.at[which], xbuf.at[which], left_send.at[which], left_recv.at[which],
            {"wide": x_mate, "narrow": 1 - narrow},
        )

    def right_copy(which, across, kind):
        to_x = 1 - x if across else x
        return remote(
            sub_ref.at[which, :, :, column_span(2 * to_x + cut)], ybuf.at[which, :, row_span(wide)],
            right_send.at[which, across, kind], right_recv.at[which, class_of[kind]],
            {"wide": 2 * level_of[kind] + to_x, "narrow": 1 - across},
        )

    def right_block(which, kind):
        return ybuf.at[which, :, row_span(2 * level_of[kind] + xor(x, 1 - narrow))]

    def right_pass(which, kind):
        block = right_block(which, 0)
        return remote(
            block, block, right_send.at[which, 1, kind], right_recv.at[which, class_of[kind]],
            {"wide": 2 * level_of[kind] + x},
        )

    def right_relay(which, kind):
        block = right_block(which, kind)
        return remote(
            block, block, relay_send.at[0, which, kind], right_recv.at[which, kind], {"wide": 2 * partner + x}
        )

    def left_own(which):
        return pltpu.make_async_copy(sub_ref.at[which], xbuf.at[which], own_sem.at[which])

    def right_own(which):
        return pltpu.make_async_copy(
            sub_ref.at[which, :, :, own_columns], ybuf.at[which, :, row_span(wide)], own_sem.at[which]
        )

    def pair_copy(which, hop):
        block = right_block(which, hop)
        return remote(block, block, pair_send.at[which, hop], pair_recv.at[which, hop], other_core)

    def b_block(which, level, far_x, far_cut):
        from_x = 1 - x if far_x else x
        from_cut = 1 - cut if far_cut else cut
        return bbuf.at[
            which, :, row_span(2 * level + xor(from_x, narrow)), column_span(2 * from_x + from_cut)
        ]

    def zb_copy(which, kind):
        block = b_block(which, z, 0, 0)
        return remote(
            block, block, zb_send.at[which, kind], zb_recv.at[which, class_of[kind]],
            {"wide": 2 * level_of[kind] + x},
        )

    def zb_relay(which, kind):
        block = b_block(which, level_of[kind], 0, 0)
        return remote(
            block, block, relay_send.at[1, which, kind], zb_recv.at[which, kind], {"wide": 2 * partner + x}
        )

    def xb_copy(which, far_cut, hop):
        block = b_block(which, level_of[hop], 0, far_cut)
        return remote(
            block, block, xb_send.at[which, far_cut, hop], xb_recv.at[which, far_cut, hop], {"wide": x_mate}
        )

    def yb_copy(which, far_x, hop):
        block = b_block(which, level_of[hop], far_x, 0)
        return remote(
            block, block, yb_send.at[which, far_x, hop], yb_recv.at[which, far_x, hop], {"cuts": 1 - cut}
        )

    def pb_copy(which, far_x, far_cut, hop):
        block = b_block(which, level_of[hop], far_x, far_cut)
        return remote(
            block, block, pb_send.at[which, far_x, far_cut, hop], pb_recv.at[which, far_x, far_cut, hop],
            other_core,
        )

    def open_exchange(which):
        launch(call(left_exchange, which), holds_left)
        guarded(holds_left, lambda: left_own(which).start())
        for kind in (3, 2, 1, 0) if which in WHOLE_WAY else (2, 1, 0):
            if kind == 0 or which not in SIDEWAYS_FIRST:
                launch(call(right_copy, which, 1, kind), holds_right)
            if kind:
                launch(call(right_copy, which, 0, kind), holds_right)
        guarded(holds_right, lambda: right_own(which).start())

    def merge(which):
        guarded(holds_left, lambda: left_own(which).wait())
        await_recv(call(left_exchange, which), holds_right)
        for hop in hops:
            await_recv(call(pair_copy, which, hop))
        left = jnp.concatenate([xbuf[which, part] for part in range(2)], axis=0)
        right = jnp.concatenate([ybuf[which, part] for part in range(2)], axis=1)
        both = jnp.dot(left, right, preferred_element_type=jnp.float32)
        real = both[:rows, :quarter] - both[rows:, quarter:]
        imag = both[:rows, quarter:] + both[rows:, :quarter]
        span = row_span(2 * z + xor(x, narrow))
        bbuf[which, 0, span, own_columns] = real.astype(jnp.bfloat16)
        bbuf[which, 1, span, own_columns] = imag.astype(jnp.bfloat16)
        for kind in (3, 2, 1) if which in LEVELS_DIRECT else (2, 1):
            launch(call(zb_copy, which, kind))
        spread(which, 0)

    def corner_copy(which, hop):
        block = b_block(which, level_of[hop], 0, 0)
        return remote(block, block, yb_send.at[which, 1, hop], yb_recv.at[which, 1, hop], corner)

    def spread(which, hop):
        if (hop, which) in CORNERS_DIRECT:
            launch(call(corner_copy, which, hop))
        launch(call(yb_copy, which, 0, hop))
        launch(call(xb_copy, which, 0, hop))
        launch(call(pb_copy, which, 0, 0, hop))

    def over_x(which, hop):
        return (hop, which) in CORNERS_OVER_X

    def take_xb(which, far_cut, hop):
        await_recv(call(xb_copy, which, far_cut, hop))
        if not far_cut and not over_x(which, hop) and (hop, which) not in CORNERS_DIRECT:
            launch(call(yb_copy, which, 1, hop))
        launch(call(pb_copy, which, 1, far_cut, hop))

    def take_yb(which, far_x, hop):
        await_recv(call(yb_copy, which, far_x, hop))
        if not far_x and over_x(which, hop):
            launch(call(xb_copy, which, 1, hop))
        launch(call(pb_copy, which, far_x, 1, hop))

    def take_sides(which, hop):
        take_xb(which, 0, hop)
        take_yb(which, 0, hop)

    def take_corner(which, hop):
        if over_x(which, hop):
            take_xb(which, 1, hop)
        else:
            take_yb(which, 1, hop)

    def take_right_piece(which, hop):
        if hop == 0:
            guarded(holds_right, lambda: right_own(which).wait())
            await_recv(call(right_copy, which, 1, 0), holds_left)
            if which in SIDEWAYS_FIRST:
                for kind in (2, 1):
                    launch(call(right_pass, which, kind), holds_left)
        else:
            await_recv(call(right_relay, which, hop))
            if hop > 1 and which not in WHOLE_WAY:
                launch(call(right_relay, which, hop), relays)
        launch(call(pair_copy, which, hop))

    def take_z(which, hop):
        await_recv(call(zb_relay, which, hop))
        if hop > 1 and which not in LEVELS_DIRECT:
            launch(call(zb_relay, which, hop), relays)
        spread(which, hop)

    near_first = list(reversed(far_first))

    def complete(which):
        for hop in hops:
            for far_x in (0, 1):
                for far_cut in (0, 1):
                    await_recv(call(pb_copy, which, far_x, far_cut, hop))

    width = dim.bit_length() - 1
    places_copy.wait()
    narrow_place = bits - 1 - (count.bit_length() - 1)

    def named_place(which, slot):
        bit = places_ref[which, slot]
        return bit + jnp.where(bit < LBITS, -lane_bits, narrow_place - LBITS)

    places = [[named_place(which, slot) for slot in range(width)] for which in range(branches)]

    def free_place(which):
        rest = bits * (bits - 1) // 2
        for slot in range(width):
            rest = rest - places[which][slot]
        return rest

    def bit_at(values, position):
        return jnp.bitwise_and(jnp.right_shift(values, position), 1)

    def gathered_place(which, values):
        found = jnp.left_shift(bit_at(values, free_place(which)), width)
        for slot in range(width):
            found = found + jnp.left_shift(
                bit_at(values, places[which][slot]), width - 1 - slot
            )
        return found

    def natural_place(which, values):
        found = jnp.left_shift(bit_at(values, width), free_place(which))
        for slot in range(width):
            found = found + jnp.left_shift(
                bit_at(values, width - 1 - slot), places[which][slot]
            )
        return found

    step = min(256, total)
    line = lax.broadcasted_iota(jnp.int32, (1, total), 1)

    def onehot(first, size, goal):
        index = lax.broadcasted_iota(jnp.int32, (size, total), 0) + first
        return (index == goal).astype(jnp.float32).astype(jnp.bfloat16)

    def product(left, right, left_axis, right_axis):
        return lax.dot_general(
            left, right, (((left_axis,), (right_axis,)), ((), ())),
            preferred_element_type=jnp.float32,
        )

    def permute(source, source_axis, goal):
        for first in range(0, total, step):
            work[first:first + step, :] = product(
                onehot(first, step, goal), source, 1, source_axis
            ).astype(jnp.bfloat16)

    def contract(which):
        branch = jnp.concatenate([bbuf[which, part] for part in range(2)], axis=1)
        for first in range(0, total, dim):
            data = work[first:first + dim, :]
            spun = jnp.concatenate([-data[:, lanes:], data[:, :lanes]], axis=1)
            both = jnp.concatenate([data, spun], axis=0)
            prod[first:first + dim, :] = jnp.dot(
                branch, both, preferred_element_type=jnp.float32
            ).astype(jnp.bfloat16)

    def swap_targets(round_no, hop):
        source, target = ((send_in, recv_in), (send_out, recv_out))[round_no]
        piece = source.shape[0] // members
        for turn in range(4):
            across, other_side = turn // 2, turn % 2
            if hop == 0 and turn == 0:
                continue
            to_x = x if across == 0 else 1 - x
            to_core = narrow if other_side == 0 else 1 - narrow
            to_wide = 2 * ahead(hop) + to_x
            other = 2 * to_wide + to_core
            yield remote(
                source.at[pl.ds(pl.multiple_of(other * piece, piece), piece)],
                target.at[pl.ds(pl.multiple_of(me * piece, piece), piece)],
                swap_send.at[round_no, 4 * hop + turn],
                swap_recv.at[round_no, 4 * hop + turn],
                {"wide": to_wide, "narrow": to_core},
            )

    def swap_start(round_no, hop):
        for copy in swap_targets(round_no, hop):
            copy.start()

    def swap_wait(round_no):
        for hop in far_first:
            for copy in swap_targets(round_no, hop):
                copy.wait_recv()

    def keep_own(source, target):
        piece = source.shape[0] // members
        mine = pl.ds(pl.multiple_of(me * piece, piece), piece)
        target[mine, :] = source[mine, :]

    def pack():
        sides = [
            stem_held[pl.ds(part, total, stride=2), :].T.reshape(members, 1, sublanes, total)
            for part in range(2)
        ]
        send_in[...] = jnp.concatenate(sides, axis=1).reshape(2 * lanes, total).astype(jnp.bfloat16)
        keep_own(send_in, recv_in)

    def arrange():
        blocks = recv_in[...].astype(jnp.float32).reshape(members, 2, sublanes, total)
        return jnp.concatenate(
            [blocks[:, part].reshape(lanes, total) for part in range(2)], axis=0
        ).astype(jnp.bfloat16)

    def mix(low, high):
        return (
            jnp.concatenate([low[..., :half], high[..., :half]], axis=-1),
            jnp.concatenate([low[..., half:], high[..., half:]], axis=-1),
        )

    def turn_over():
        goal = natural_place(0, line)
        for first in range(0, total, step):
            turned[:, first:first + step] = product(prod[...], onehot(first, step, goal), 0, 1)
        for tile in range(tiles):
            block = turned[:, tile * lanes:(tile + 1) * lanes].reshape(2, count, 2, sublanes, lanes)
            for side, mixed in enumerate(mix(block[:, :, 0], block[:, :, 1])):
                for part in range(2):
                    first = ((part * 2 + side) * tiles + tile) * sublanes
                    flipped[first:first + sublanes, :] = jnp.concatenate(
                        [mixed[part, column] for column in range(count)], axis=1
                    )

    def hand_out(hop, goal):
        span = 2 * lanes
        first = ahead(hop) * span
        level = product(prod[...], onehot(first, span, goal), 0, 1)
        piece = send_out.shape[0] // members
        for to_x in range(2):
            block = level[:, to_x * lanes:(to_x + 1) * lanes].reshape(2, 2, half, lanes)
            for side, mixed in enumerate(mix(block[:, 0], block[:, 1])):
                other = 2 * (2 * ahead(hop) + to_x) + side
                send_out[pl.ds(pl.multiple_of(other * piece, piece), piece), :] = mixed.reshape(
                    piece, lanes
                ).astype(jnp.bfloat16)
        swap_start(1, hop)

    stem_copy.wait()
    pack()
    pl.semaphore_wait(barrier, members + 1)
    swap_start(0, 1)
    open_exchange(1)
    take_right_piece(1, 0)
    open_exchange(0)
    open_exchange(2)
    take_right_piece(1, 3)
    take_right_piece(1, 2)
    take_right_piece(1, 1)
    take_right_piece(2, 0)
    merge(1)
    take_right_piece(0, 0)
    take_right_piece(0, 1)
    take_right_piece(0, 3)
    take_right_piece(0, 2)
    take_right_piece(2, 1)
    merge(0)
    take_right_piece(2, 2)
    take_right_piece(2, 3)
    take_z(1, 2)
    merge(2)
    take_z(0, 2)
    take_z(1, 3)
    take_sides(0, 0)
    take_z(2, 2)
    take_z(1, 1)
    take_sides(1, 2)
    take_z(0, 3)
    take_sides(0, 2)
    take_z(0, 1)
    take_sides(2, 2)
    take_z(2, 1)
    swap_start(0, 2)
    take_sides(1, 0)
    take_sides(1, 1)
    take_sides(1, 3)
    take_corner(0, 0)
    take_z(2, 3)
    take_corner(0, 2)
    swap_start(0, 3)
    swap_start(0, 0)
    take_sides(0, 1)
    take_sides(0, 3)
    take_sides(2, 1)
    take_corner(0, 1)
    take_corner(1, 0)
    take_sides(2, 0)
    take_corner(0, 3)
    take_corner(2, 2)
    take_sides(2, 3)
    take_corner(1, 1)
    take_corner(2, 1)
    take_corner(1, 2)
    take_corner(1, 3)
    complete(0)
    swap_wait(0)
    permute(arrange(), 1, gathered_place(0, line))
    contract(0)
    turn_over()
    take_corner(2, 3)
    take_corner(2, 0)
    complete(1)
    permute(flipped[...].astype(jnp.bfloat16), 1, gathered_place(1, line))
    contract(1)
    permute(prod[...], 0, gathered_place(2, natural_place(1, line)))
    complete(2)
    contract(2)
    goal = natural_place(2, line)
    for hop in far_first:
        hand_out(hop, goal)
    keep_own(send_out, recv_out)
    swap_wait(1)
    out_ref[...] = recv_out[...]


    for hop in hops:
        for round_no in range(2):
            for copy in swap_targets(round_no, hop):
                copy.wait_send()
    for build, guard in started:
        guarded(guard, lambda: build().wait_send())


def write_kernel(parts_ref, out_ref, held, sems):
    lanes = held.shape[1]
    members = parts_ref.shape[0] // lanes
    tiles = lanes // (2 * sublanes)
    copies = []
    for tile in range(tiles):
        for part in range(2):
            first = (part * tiles + tile) * sublanes
            start = first // 16 * 16
            block = jnp.concatenate(
                [
                    parts_ref[member * lanes + start:member * lanes + start + 16, :].astype(jnp.float32)[
                        first - start:first - start + sublanes
                    ]
                    for member in range(members)
                ],
                axis=0,
            )
            held[pl.ds(2 * tile * lanes + part, lanes, stride=2), :] = block.T
        span = pl.ds(2 * tile * lanes, 2 * lanes)
        copies.append(pltpu.make_async_copy(held.at[span], out_ref.at[span], sems.at[tile]))
        copies[-1].start()
    for copy in copies:
        copy.wait()


def shards_in_kernel(stem_tensor, sub_branches, branch_bits):
    count = lax.axis_size("wide")
    depth = count // 2
    lanes = 2**lane_bits
    total = stem_tensor.shape[1] // lanes
    dim = sub_branches.shape[-1]
    stem = stem_tensor.reshape(2, total, lanes).transpose(1, 0, 2).reshape(2 * total, lanes)
    vmem = pl.BlockSpec(memory_space=pltpu.VMEM)
    hbm = pl.BlockSpec(memory_space=pl.ANY)
    each = (BRANCHES, depth)
    semaphores = [pltpu.SemaphoreType.DMA(()), pltpu.SemaphoreType.DMA((BRANCHES,))]
    for sent, received in (
        ((BRANCHES,), (BRANCHES,)), ((BRANCHES, 2, depth), each), (each, each), (each, each),
        ((BRANCHES, 2, depth),) * 2, ((BRANCHES, 2, depth),) * 2, ((BRANCHES, 2, 2, depth),) * 2, ((2, 2 * count),) * 2,
    ):
        semaphores += [pltpu.SemaphoreType.DMA(sent), pltpu.SemaphoreType.DMA(received)]
    semaphores.insert(8, pltpu.SemaphoreType.DMA((2,) + each))
    half_size = jnp.bfloat16
    result = pl.pallas_call(
        functools.partial(stem_kernel, count),
        out_shape=jax.ShapeDtypeStruct((2 * total, lanes), half_size),
        in_specs=[pl.BlockSpec(memory_space=pltpu.MemorySpace.HBM), hbm, hbm],
        out_specs=vmem,
        scratch_shapes=[
            pltpu.SMEM(branch_bits.shape, jnp.int32),
            pltpu.SemaphoreType.DMA(()),
            pltpu.VMEM((BRANCHES,) + sub_branches.shape[2:], half_size),
            pltpu.VMEM((BRANCHES, 2, dim, dim // 4), half_size),
            pltpu.VMEM((BRANCHES, 2, dim, dim), half_size),
            pltpu.VMEM((total, 2 * lanes), half_size),
            pltpu.VMEM((total, 2 * lanes), half_size),
            pltpu.VMEM((2 * lanes, total), jnp.float32),
            pltpu.VMEM((2 * lanes, total), jnp.float32),
            pltpu.VMEM((2 * lanes, total), half_size),
            pltpu.VMEM((2 * lanes, total), half_size),
            pltpu.VMEM((2 * total, lanes), half_size),
            pltpu.VMEM((2 * total, lanes), half_size),
            pltpu.VMEM((2 * total, lanes), jnp.float32),
        ] + semaphores,
        compiler_params=pltpu.CompilerParams(
            collective_id=0, has_side_effects=True, vmem_limit_bytes=kernel_vmem
        ),
    )(*[pltpu.with_memory_space_constraint(v, pltpu.MemorySpace.HBM) for v in (branch_bits, stem, sub_branches[:, 0])])
    result = pl.pallas_call(
        write_kernel,
        out_shape=jax.ShapeDtypeStruct((2 * total, lanes), jnp.float32),
        in_specs=[vmem],
        out_specs=hbm,
        scratch_shapes=[
            pltpu.VMEM((2 * total, lanes), jnp.float32), pltpu.SemaphoreType.DMA((total // lanes,))
        ],
        compiler_params=pltpu.CompilerParams(vmem_limit_bytes=kernel_vmem),
    )(result)
    return result.reshape(total, 2, lanes).transpose(1, 0, 2).reshape(2, -1)


sublane_tile = 16


def solution(mesh):
    in_specs = (P(None, ("cuts", "wide", "narrow")), P(None, "narrow", None, "wide", None), P())
    out_specs = P(None, ("cuts", "wide", "narrow"))

    def run(stem_tensor, sub_branches, branch_bits):
        whole_tiles = sub_branches.shape[3] % sublane_tile == 0 and mesh.shape["cuts"] == 2
        whole_groups = 2 * mesh.shape["wide"] * sublanes == 2**lane_bits
        body = shards_in_kernel if whole_tiles and whole_groups else shards
        return body(stem_tensor, sub_branches, branch_bits)

    return jax.shard_map(run, mesh=mesh, in_specs=in_specs, out_specs=out_specs, check_vma=False)
```

```python
import functools

import jax
import jax.numpy as jnp
from jax import lax
from jax.experimental import pallas as pl
from jax.experimental.pallas import tpu as pltpu
from jax.sharding import PartitionSpec as P

LBITS = 17
BBITS = 9
BRANCHES = 3


lane_bits = 7
sublanes = 8
kernel_vmem = 32 * 2**20
CORNERS_OVER_X = ((2, 0), (2, 2))
WHOLE_WAY = ()
SIDEWAYS_FIRST = ()
CORNERS_DIRECT = ()
LEVELS_DIRECT = ()


def partner(value, axis, stride):
    mask = 2**stride
    pairs = [(source, source ^ mask) for source in range(lax.axis_size(axis))]
    return lax.ppermute(value, axis, pairs)


def bit_tables(chosen_bits, total_bits, width_bits):
    places = jnp.arange(total_bits, dtype=jnp.int32)
    orders = jnp.arange(width_bits, dtype=jnp.int32)
    matches = places[:, None] == chosen_bits[None, :]
    chosen = jnp.any(matches, axis=1)
    ranking = jnp.sum(jnp.where(matches, orders[None, :], 0), axis=1)
    unchosen = 1 - chosen.astype(jnp.int32)
    free_rank = jnp.cumsum(unchosen) - unchosen
    unit_ones = jnp.ones((total_bits,), jnp.int32)
    weight = jnp.where(
        chosen,
        jnp.left_shift(unit_ones, width_bits - 1 - ranking),
        jnp.left_shift(unit_ones, width_bits + free_rank),
    )
    low_bits = total_bits // 2

    def partial_table(count, first_place, last_place):
        values = jnp.arange(count, dtype=jnp.int32)
        running = jnp.zeros((count,), jnp.int32)
        for position in range(first_place, last_place):
            running = (
                running
                + jnp.bitwise_and(jnp.right_shift(values, position - first_place), 1)
                * weight[position]
            )
        return running

    inverse = (
        partial_table(2 ** (total_bits - low_bits), low_bits, total_bits)[:, None]
        + partial_table(2**low_bits, 0, low_bits)[None, :]
    ).reshape(-1)
    columns = jnp.arange(2**width_bits, dtype=jnp.int32)
    col_part = jnp.zeros((2**width_bits,), jnp.int32)
    for slot_no in range(width_bits):
        col_part = col_part + jnp.left_shift(
            jnp.bitwise_and(jnp.right_shift(columns, width_bits - 1 - slot_no), 1),
            chosen_bits[slot_no],
        )
    row_ids = jnp.arange(2 ** (total_bits - width_bits), dtype=jnp.int32)
    row_part = jnp.zeros((2 ** (total_bits - width_bits),), jnp.int32)
    for position in range(total_bits):
        bit_value = jnp.bitwise_and(jnp.right_shift(row_ids, free_rank[position]), 1) * 2**position
        row_part = row_part + jnp.where(chosen[position], 0, bit_value)
    gather_index = row_part[:, None] + col_part[None, :]
    return (gather_index, inverse)


def half_product(first_matrix, second_matrix):
    return jnp.dot(first_matrix, second_matrix, preferred_element_type=jnp.float32)


def merge_branch(left_factor, right_factor):
    real_part = half_product(left_factor[0], right_factor[0]) - half_product(
        left_factor[1], right_factor[1]
    )
    imag_part = half_product(left_factor[0], right_factor[1]) + half_product(
        left_factor[1], right_factor[0]
    )
    return jnp.stack([real_part, imag_part]).astype(jnp.bfloat16)


def contract_blocks(amplitude, branch, gather_index, inverse):
    lanes = 2**lane_bits
    blocks = amplitude.reshape(2, -1, lanes)
    picked = jnp.take(blocks, gather_index, axis=1)
    widened = branch.astype(jnp.float32)

    def real_product(data, matrix):
        return jnp.einsum(
            "rul,cu->rcl",
            data,
            matrix,
            precision=lax.Precision.HIGHEST,
            preferred_element_type=jnp.float32,
        )

    real_part = real_product(picked[0], widened[0]) - real_product(picked[1], widened[1])
    imag_part = real_product(picked[0], widened[1]) + real_product(picked[1], widened[0])
    merged = jnp.stack([real_part, imag_part]).reshape(2, -1, lanes)
    return jnp.take(merged, inverse, axis=1).reshape(2, -1)


def shards(stem_tensor, sub_branches, branch_bits):
    wide_count = lax.axis_size("wide")
    wide_log = wide_count.bit_length() - 1
    local_bits = LBITS
    block_shape = (2, wide_count, 2, stem_tensor.shape[1] // (2 * wide_count))
    leading = lax.axis_index("narrow") == 0

    def move_wide(amplitude):
        return lax.all_to_all(
            amplitude.reshape(block_shape), "wide", split_axis=1, concat_axis=1, tiled=True
        ).reshape(2, -1)

    def move_narrow(amplitude):
        return lax.all_to_all(
            amplitude.reshape(block_shape), "narrow", split_axis=2, concat_axis=2, tiled=True
        ).reshape(2, -1)

    def working_places(which):
        chosen_bits = branch_bits[which]
        if which == 0:
            return chosen_bits - lane_bits
        shifted = jnp.where(chosen_bits == local_bits, local_bits - wide_log - 1, chosen_bits)
        placed = jnp.where(chosen_bits > local_bits, chosen_bits - wide_log - 1, shifted)
        return placed - lane_bits

    amplitude = stem_tensor
    for which in range(BRANCHES):
        own_rows = sub_branches[which, 0]
        own_whole = lax.all_gather(own_rows, "wide", axis=1, tiled=True)
        partner_whole = partner(own_whole, "narrow", 0)
        branch = merge_branch(
            jnp.where(leading, own_whole, partner_whole),
            jnp.where(leading, partner_whole, own_whole),
        )
        if which == 1:
            amplitude = move_wide(amplitude)
        if which == 2:
            amplitude = move_narrow(amplitude)
        gather_index, inverse = bit_tables(working_places(which), local_bits - lane_bits, BBITS)
        amplitude = contract_blocks(amplitude, branch, gather_index, inverse)
    amplitude = move_narrow(amplitude)
    amplitude = move_wide(amplitude)
    return amplitude


MESH = pl.DeviceIdType.MESH


def xor(first, second):
    return first + second - 2 * first * second


def stem_kernel(
    count, bits_ref, stem_ref, sub_ref, out_ref, places_ref, places_sem,
    xbuf, ybuf, bbuf, work, prod, turned, flipped, send_in, recv_in, send_out, recv_out, stem_held,
    stem_sem, own_sem, left_send, left_recv, right_send, right_recv, pair_send, pair_recv,
    relay_send, zb_send, zb_recv, xb_send, xb_recv, yb_send, yb_recv, pb_send, pb_recv,
    swap_send, swap_recv,
):
    wide = lax.axis_index("wide")
    narrow = lax.axis_index("narrow")
    cut = lax.axis_index("cuts")
    rows = sub_ref.shape[2]
    branches = sub_ref.shape[0]
    dim = bbuf.shape[2]
    quarter = dim // 4
    total = work.shape[0]
    lanes = work.shape[1] // 2
    bits = total.bit_length() - 1
    depth = count // 2
    z = wide // 2
    x = wide % 2
    members = 2 * count
    me = wide * 2 + narrow
    x_mate = 2 * z + 1 - x
    half = lanes // 2
    tiles = total // lanes

    stem_copy = pltpu.make_async_copy(stem_ref, stem_held, stem_sem)
    stem_copy.start()
    places_copy = pltpu.make_async_copy(bits_ref, places_ref, places_sem)
    places_copy.start()
    barrier = pltpu.get_barrier_semaphore()
    for step in sorted(range(1, members), key=lambda step: -min(step, members - step)):
        other = lax.rem(me + step, members)
        pl.semaphore_signal(
            barrier, inc=1, device_id={"wide": other // 2, "narrow": other % 2}, device_id_type=MESH
        )
    corner = {"wide": x_mate, "cuts": 1 - cut}
    for target in ({"cuts": 1 - cut}, corner):
        pl.semaphore_signal(barrier, inc=1, device_id=target, device_id_type=MESH)

    started = []
    call = functools.partial
    hops = range(depth)
    far_first = sorted(hops, key=lambda hop: -min(hop, depth - hop))

    def ahead(hop):
        return (z + hop) % depth

    side = z // (depth // 2)
    partner = z + 1 - 2 * (z % 2)
    inner = (z + side) % 2
    level_of = (z, partner, depth // 2 - side, (depth - 1) * (1 - side))
    far_class = 3 - inner
    class_of = (0, 1, far_class, far_class)
    relays = inner == 1

    def row_span(block):
        return pl.ds(pl.multiple_of(block * rows, rows), rows)

    def column_span(block):
        return pl.ds(pl.multiple_of(block * quarter, quarter), quarter)

    def remote(src, dst, send_sem, recv_sem, device_id):
        return pltpu.make_async_remote_copy(
            src_ref=src, dst_ref=dst, send_sem=send_sem, recv_sem=recv_sem,
            device_id=device_id, device_id_type=MESH,
        )

    def guarded(guard, action):
        if guard is None:
            action()
        else:
            pl.when(guard)(action)

    def launch(build, guard=None):
        guarded(guard, lambda: build().start())
        started.append((build, guard))

    def await_recv(build, guard=None):
        guarded(guard, lambda: build().wait_recv())

    holds_left = narrow == 0
    holds_right = narrow == 1
    other_core = {"narrow": 1 - narrow}
    own_columns = column_span(2 * x + cut)

    def left_exchange(which):
        return remote(
            sub_ref.at[which], xbuf.at[which], left_send.at[which], left_recv.at[which],
            {"wide": x_mate, "narrow": 1 - narrow},
        )

    def right_copy(which, across, kind):
        to_x = 1 - x if across else x
        return remote(
            sub_ref.at[which, :, :, column_span(2 * to_x + cut)], ybuf.at[which, :, row_span(wide)],
            right_send.at[which, across, kind], right_recv.at[which, class_of[kind]],
            {"wide": 2 * level_of[kind] + to_x, "narrow": 1 - across},
        )

    def right_block(which, kind):
        return ybuf.at[which, :, row_span(2 * level_of[kind] + xor(x, 1 - narrow))]

    def right_pass(which, kind):
        block = right_block(which, 0)
        return remote(
            block, block, right_send.at[which, 1, kind], right_recv.at[which, class_of[kind]],
            {"wide": 2 * level_of[kind] + x},
        )

    def right_relay(which, kind):
        block = right_block(which, kind)
        return remote(
            block, block, relay_send.at[0, which, kind], right_recv.at[which, kind], {"wide": 2 * partner + x}
        )

    def left_own(which):
        return pltpu.make_async_copy(sub_ref.at[which], xbuf.at[which], own_sem.at[which])

    def right_own(which):
        return pltpu.make_async_copy(
            sub_ref.at[which, :, :, own_columns], ybuf.at[which, :, row_span(wide)], own_sem.at[which]
        )

    def pair_copy(which, hop):
        block = right_block(which, hop)
        return remote(block, block, pair_send.at[which, hop], pair_recv.at[which, hop], other_core)

    def b_block(which, level, far_x, far_cut):
        from_x = 1 - x if far_x else x
        from_cut = 1 - cut if far_cut else cut
        return bbuf.at[
            which, :, row_span(2 * level + xor(from_x, narrow)), column_span(2 * from_x + from_cut)
        ]

    def zb_copy(which, kind):
        block = b_block(which, z, 0, 0)
        return remote(
            block, block, zb_send.at[which, kind], zb_recv.at[which, class_of[kind]],
            {"wide": 2 * level_of[kind] + x},
        )

    def zb_relay(which, kind):
        block = b_block(which, level_of[kind], 0, 0)
        return remote(
            block, block, relay_send.at[1, which, kind], zb_recv.at[which, kind], {"wide": 2 * partner + x}
        )

    def xb_copy(which, far_cut, hop):
        block = b_block(which, level_of[hop], 0, far_cut)
        return remote(
            block, block, xb_send.at[which, far_cut, hop], xb_recv.at[which, far_cut, hop], {"wide": x_mate}
        )

    def yb_copy(which, far_x, hop):
        block = b_block(which, level_of[hop], far_x, 0)
        return remote(
            block, block, yb_send.at[which, far_x, hop], yb_recv.at[which, far_x, hop], {"cuts": 1 - cut}
        )

    def pb_copy(which, far_x, far_cut, hop):
        block = b_block(which, level_of[hop], far_x, far_cut)
        return remote(
            block, block, pb_send.at[which, far_x, far_cut, hop], pb_recv.at[which, far_x, far_cut, hop],
            other_core,
        )

    def open_exchange(which):
        launch(call(left_exchange, which), holds_left)
        guarded(holds_left, lambda: left_own(which).start())
        for kind in (3, 2, 1, 0) if which in WHOLE_WAY else (2, 1, 0):
            if kind == 0 or which not in SIDEWAYS_FIRST:
                launch(call(right_copy, which, 1, kind), holds_right)
            if kind:
                launch(call(right_copy, which, 0, kind), holds_right)
        guarded(holds_right, lambda: right_own(which).start())

    def merge(which):
        guarded(holds_left, lambda: left_own(which).wait())
        await_recv(call(left_exchange, which), holds_right)
        for hop in hops:
            await_recv(call(pair_copy, which, hop))
        left = jnp.concatenate([xbuf[which, part] for part in range(2)], axis=0)
        right = jnp.concatenate([ybuf[which, part] for part in range(2)], axis=1)
        both = jnp.dot(left, right, preferred_element_type=jnp.float32)
        real = both[:rows, :quarter] - both[rows:, quarter:]
        imag = both[:rows, quarter:] + both[rows:, :quarter]
        span = row_span(2 * z + xor(x, narrow))
        bbuf[which, 0, span, own_columns] = real.astype(jnp.bfloat16)
        bbuf[which, 1, span, own_columns] = imag.astype(jnp.bfloat16)
        for kind in (3, 2, 1) if which in LEVELS_DIRECT else (2, 1):
            launch(call(zb_copy, which, kind))
        spread(which, 0)

    def corner_copy(which, hop):
        block = b_block(which, level_of[hop], 0, 0)
        return remote(block, block, yb_send.at[which, 1, hop], yb_recv.at[which, 1, hop], corner)

    def spread(which, hop):
        if (hop, which) in CORNERS_DIRECT:
            launch(call(corner_copy, which, hop))
        launch(call(yb_copy, which, 0, hop))
        launch(call(xb_copy, which, 0, hop))
        launch(call(pb_copy, which, 0, 0, hop))

    def over_x(which, hop):
        return (hop, which) in CORNERS_OVER_X

    def take_xb(which, far_cut, hop):
        await_recv(call(xb_copy, which, far_cut, hop))
        if not far_cut and not over_x(which, hop) and (hop, which) not in CORNERS_DIRECT:
            launch(call(yb_copy, which, 1, hop))
        launch(call(pb_copy, which, 1, far_cut, hop))

    def take_yb(which, far_x, hop):
        await_recv(call(yb_copy, which, far_x, hop))
        if not far_x and over_x(which, hop):
            launch(call(xb_copy, which, 1, hop))
        launch(call(pb_copy, which, far_x, 1, hop))

    def take_sides(which, hop):
        take_xb(which, 0, hop)
        take_yb(which, 0, hop)

    def take_corner(which, hop):
        if over_x(which, hop):
            take_xb(which, 1, hop)
        else:
            take_yb(which, 1, hop)

    def take_right_piece(which, hop):
        if hop == 0:
            guarded(holds_right, lambda: right_own(which).wait())
            await_recv(call(right_copy, which, 1, 0), holds_left)
            if which in SIDEWAYS_FIRST:
                for kind in (2, 1):
                    launch(call(right_pass, which, kind), holds_left)
        else:
            await_recv(call(right_relay, which, hop))
            if hop > 1 and which not in WHOLE_WAY:
                launch(call(right_relay, which, hop), relays)
        launch(call(pair_copy, which, hop))

    def take_z(which, hop):
        await_recv(call(zb_relay, which, hop))
        if hop > 1 and which not in LEVELS_DIRECT:
            launch(call(zb_relay, which, hop), relays)
        spread(which, hop)

    near_first = list(reversed(far_first))

    def complete(which):
        for hop in hops:
            for far_x in (0, 1):
                for far_cut in (0, 1):
                    await_recv(call(pb_copy, which, far_x, far_cut, hop))

    width = dim.bit_length() - 1
    places_copy.wait()
    narrow_place = bits - 1 - (count.bit_length() - 1)

    def named_place(which, slot):
        bit = places_ref[which, slot]
        return bit + jnp.where(bit < LBITS, -lane_bits, narrow_place - LBITS)

    places = [[named_place(which, slot) for slot in range(width)] for which in range(branches)]

    def free_place(which):
        rest = bits * (bits - 1) // 2
        for slot in range(width):
            rest = rest - places[which][slot]
        return rest

    def bit_at(values, position):
        return jnp.bitwise_and(jnp.right_shift(values, position), 1)

    def gathered_place(which, values):
        found = jnp.left_shift(bit_at(values, free_place(which)), width)
        for slot in range(width):
            found = found + jnp.left_shift(
                bit_at(values, places[which][slot]), width - 1 - slot
            )
        return found

    def natural_place(which, values):
        found = jnp.left_shift(bit_at(values, width), free_place(which))
        for slot in range(width):
            found = found + jnp.left_shift(
                bit_at(values, width - 1 - slot), places[which][slot]
            )
        return found

    step = min(256, total)
    line = lax.broadcasted_iota(jnp.int32, (1, total), 1)

    def onehot(first, size, goal):
        index = lax.broadcasted_iota(jnp.int32, (size, total), 0) + first
        return (index == goal).astype(jnp.float32).astype(jnp.bfloat16)

    def product(left, right, left_axis, right_axis):
        return lax.dot_general(
            left, right, (((left_axis,), (right_axis,)), ((), ())),
            preferred_element_type=jnp.float32,
        )

    def permute(source, source_axis, goal):
        for first in range(0, total, step):
            work[first:first + step, :] = product(
                onehot(first, step, goal), source, 1, source_axis
            ).astype(jnp.bfloat16)

    def contract(which):
        branch = jnp.concatenate([bbuf[which, part] for part in range(2)], axis=1)
        for first in range(0, total, dim):
            data = work[first:first + dim, :]
            spun = jnp.concatenate([-data[:, lanes:], data[:, :lanes]], axis=1)
            both = jnp.concatenate([data, spun], axis=0)
            prod[first:first + dim, :] = jnp.dot(
                branch, both, preferred_element_type=jnp.float32
            ).astype(jnp.bfloat16)

    def swap_targets(round_no, hop):
        source, target = ((send_in, recv_in), (send_out, recv_out))[round_no]
        piece = source.shape[0] // members
        for turn in range(4):
            across, other_side = turn // 2, turn % 2
            if hop == 0 and turn == 0:
                continue
            to_x = x if across == 0 else 1 - x
            to_core = narrow if other_side == 0 else 1 - narrow
            to_wide = 2 * ahead(hop) + to_x
            other = 2 * to_wide + to_core
            yield remote(
                source.at[pl.ds(pl.multiple_of(other * piece, piece), piece)],
                target.at[pl.ds(pl.multiple_of(me * piece, piece), piece)],
                swap_send.at[round_no, 4 * hop + turn],
                swap_recv.at[round_no, 4 * hop + turn],
                {"wide": to_wide, "narrow": to_core},
            )

    def swap_start(round_no, hop):
        for copy in swap_targets(round_no, hop):
            copy.start()

    def swap_wait(round_no):
        for hop in far_first:
            for copy in swap_targets(round_no, hop):
                copy.wait_recv()

    def keep_own(source, target):
        piece = source.shape[0] // members
        mine = pl.ds(pl.multiple_of(me * piece, piece), piece)
        target[mine, :] = source[mine, :]

    def pack():
        sides = [
            stem_held[pl.ds(part, total, stride=2), :].T.reshape(members, 1, sublanes, total)
            for part in range(2)
        ]
        send_in[...] = jnp.concatenate(sides, axis=1).reshape(2 * lanes, total).astype(jnp.bfloat16)
        keep_own(send_in, recv_in)

    def arrange():
        blocks = recv_in[...].astype(jnp.float32).reshape(members, 2, sublanes, total)
        return jnp.concatenate(
            [blocks[:, part].reshape(lanes, total) for part in range(2)], axis=0
        ).astype(jnp.bfloat16)

    def mix(low, high):
        return (
            jnp.concatenate([low[..., :half], high[..., :half]], axis=-1),
            jnp.concatenate([low[..., half:], high[..., half:]], axis=-1),
        )

    def turn_over():
        goal = natural_place(0, line)
        for first in range(0, total, step):
            turned[:, first:first + step] = product(prod[...], onehot(first, step, goal), 0, 1)
        for tile in range(tiles):
            block = turned[:, tile * lanes:(tile + 1) * lanes].reshape(2, count, 2, sublanes, lanes)
            for side, mixed in enumerate(mix(block[:, :, 0], block[:, :, 1])):
                for part in range(2):
                    first = ((part * 2 + side) * tiles + tile) * sublanes
                    flipped[first:first + sublanes, :] = jnp.concatenate(
                        [mixed[part, column] for column in range(count)], axis=1
                    )

    def hand_out(hop, goal):
        span = 2 * lanes
        first = ahead(hop) * span
        level = product(prod[...], onehot(first, span, goal), 0, 1)
        piece = send_out.shape[0] // members
        for to_x in range(2):
            block = level[:, to_x * lanes:(to_x + 1) * lanes].reshape(2, 2, half, lanes)
            for side, mixed in enumerate(mix(block[:, 0], block[:, 1])):
                other = 2 * (2 * ahead(hop) + to_x) + side
                send_out[pl.ds(pl.multiple_of(other * piece, piece), piece), :] = mixed.reshape(
                    piece, lanes
                ).astype(jnp.bfloat16)
        swap_start(1, hop)

    stem_copy.wait()
    pack()
    pl.semaphore_wait(barrier, members + 1)
    swap_start(0, 1)
    open_exchange(1)
    take_right_piece(1, 0)
    open_exchange(0)
    open_exchange(2)
    take_right_piece(1, 3)
    take_right_piece(1, 2)
    take_right_piece(1, 1)
    take_right_piece(2, 0)
    merge(1)
    take_right_piece(0, 0)
    take_right_piece(0, 1)
    take_right_piece(0, 3)
    take_right_piece(0, 2)
    take_right_piece(2, 1)
    merge(0)
    take_right_piece(2, 2)
    take_right_piece(2, 3)
    take_z(1, 2)
    merge(2)
    take_z(0, 2)
    take_z(1, 3)
    take_sides(0, 0)
    take_z(2, 2)
    take_z(1, 1)
    take_sides(1, 2)
    take_z(0, 3)
    take_sides(0, 2)
    take_z(0, 1)
    take_sides(2, 2)
    take_z(2, 1)
    swap_start(0, 2)
    take_sides(1, 0)
    take_sides(1, 1)
    take_sides(1, 3)
    take_corner(0, 0)
    take_z(2, 3)
    take_corner(0, 2)
    swap_start(0, 3)
    swap_start(0, 0)
    take_sides(0, 1)
    take_sides(0, 3)
    take_sides(2, 1)
    take_corner(0, 1)
    take_corner(1, 0)
    take_sides(2, 0)
    take_corner(0, 3)
    take_corner(2, 2)
    take_sides(2, 3)
    take_corner(1, 1)
    take_corner(2, 1)
    take_corner(1, 2)
    take_corner(1, 3)
    complete(0)
    swap_wait(0)
    permute(arrange(), 1, gathered_place(0, line))
    contract(0)
    turn_over()
    permute(flipped[...].astype(jnp.bfloat16), 1, gathered_place(1, line))
    take_corner(2, 3)
    take_corner(2, 0)
    complete(1)
    contract(1)
    permute(prod[...], 0, gathered_place(2, natural_place(1, line)))
    complete(2)
    contract(2)
    goal = natural_place(2, line)
    for hop in far_first:
        hand_out(hop, goal)
    keep_own(send_out, recv_out)
    swap_wait(1)
    out_ref[...] = recv_out[...]


    for hop in hops:
        for round_no in range(2):
            for copy in swap_targets(round_no, hop):
                copy.wait_send()
    for build, guard in started:
        guarded(guard, lambda: build().wait_send())


def write_kernel(parts_ref, out_ref, held, sems):
    lanes = held.shape[1]
    members = parts_ref.shape[0] // lanes
    tiles = lanes // (2 * sublanes)
    copies = []
    for tile in range(tiles):
        for part in range(2):
            first = (part * tiles + tile) * sublanes
            start = first // 16 * 16
            block = jnp.concatenate(
                [
                    parts_ref[member * lanes + start:member * lanes + start + 16, :].astype(jnp.float32)[
                        first - start:first - start + sublanes
                    ]
                    for member in range(members)
                ],
                axis=0,
            )
            held[pl.ds(2 * tile * lanes + part, lanes, stride=2), :] = block.T
        span = pl.ds(2 * tile * lanes, 2 * lanes)
        copies.append(pltpu.make_async_copy(held.at[span], out_ref.at[span], sems.at[tile]))
        copies[-1].start()
    for copy in copies:
        copy.wait()


def shards_in_kernel(stem_tensor, sub_branches, branch_bits):
    count = lax.axis_size("wide")
    depth = count // 2
    lanes = 2**lane_bits
    total = stem_tensor.shape[1] // lanes
    dim = sub_branches.shape[-1]
    stem = stem_tensor.reshape(2, total, lanes).transpose(1, 0, 2).reshape(2 * total, lanes)
    vmem = pl.BlockSpec(memory_space=pltpu.VMEM)
    hbm = pl.BlockSpec(memory_space=pl.ANY)
    each = (BRANCHES, depth)
    semaphores = [pltpu.SemaphoreType.DMA(()), pltpu.SemaphoreType.DMA((BRANCHES,))]
    for sent, received in (
        ((BRANCHES,), (BRANCHES,)), ((BRANCHES, 2, depth), each), (each, each), (each, each),
        ((BRANCHES, 2, depth),) * 2, ((BRANCHES, 2, depth),) * 2, ((BRANCHES, 2, 2, depth),) * 2, ((2, 2 * count),) * 2,
    ):
        semaphores += [pltpu.SemaphoreType.DMA(sent), pltpu.SemaphoreType.DMA(received)]
    semaphores.insert(8, pltpu.SemaphoreType.DMA((2,) + each))
    half_size = jnp.bfloat16
    result = pl.pallas_call(
        functools.partial(stem_kernel, count),
        out_shape=jax.ShapeDtypeStruct((2 * total, lanes), half_size),
        in_specs=[pl.BlockSpec(memory_space=pltpu.MemorySpace.HBM), hbm, hbm],
        out_specs=vmem,
        scratch_shapes=[
            pltpu.SMEM(branch_bits.shape, jnp.int32),
            pltpu.SemaphoreType.DMA(()),
            pltpu.VMEM((BRANCHES,) + sub_branches.shape[2:], half_size),
            pltpu.VMEM((BRANCHES, 2, dim, dim // 4), half_size),
            pltpu.VMEM((BRANCHES, 2, dim, dim), half_size),
            pltpu.VMEM((total, 2 * lanes), half_size),
            pltpu.VMEM((total, 2 * lanes), half_size),
            pltpu.VMEM((2 * lanes, total), jnp.float32),
            pltpu.VMEM((2 * lanes, total), jnp.float32),
            pltpu.VMEM((2 * lanes, total), half_size),
            pltpu.VMEM((2 * lanes, total), half_size),
            pltpu.VMEM((2 * total, lanes), half_size),
            pltpu.VMEM((2 * total, lanes), half_size),
            pltpu.VMEM((2 * total, lanes), jnp.float32),
        ] + semaphores,
        compiler_params=pltpu.CompilerParams(
            collective_id=0, has_side_effects=True, vmem_limit_bytes=kernel_vmem
        ),
    )(*[pltpu.with_memory_space_constraint(v, pltpu.MemorySpace.HBM) for v in (branch_bits, stem, sub_branches[:, 0])])
    result = pl.pallas_call(
        write_kernel,
        out_shape=jax.ShapeDtypeStruct((2 * total, lanes), jnp.float32),
        in_specs=[vmem],
        out_specs=hbm,
        scratch_shapes=[
            pltpu.VMEM((2 * total, lanes), jnp.float32), pltpu.SemaphoreType.DMA((total // lanes,))
        ],
        compiler_params=pltpu.CompilerParams(vmem_limit_bytes=kernel_vmem),
    )(result)
    return result.reshape(total, 2, lanes).transpose(1, 0, 2).reshape(2, -1)


sublane_tile = 16


def solution(mesh):
    in_specs = (P(None, ("cuts", "wide", "narrow")), P(None, "narrow", None, "wide", None), P())
    out_specs = P(None, ("cuts", "wide", "narrow"))

    def run(stem_tensor, sub_branches, branch_bits):
        whole_tiles = sub_branches.shape[3] % sublane_tile == 0 and mesh.shape["cuts"] == 2
        whole_groups = 2 * mesh.shape["wide"] * sublanes == 2**lane_bits
        body = shards_in_kernel if whole_tiles and whole_groups else shards
        return body(stem_tensor, sub_branches, branch_bits)

    return jax.shard_map(run, mesh=mesh, in_specs=in_specs, out_specs=out_specs, check_vma=False)
```
